256 devices in a mesh: row: 8 (over z), col: 32 (over x, y, core).
Axes of the slice: x: 4, y: 4, z: 8, core: 2. Of those that a mesh axis runs over, the one named last changes fastest.
Arguments:
- three_index: float32 [256, 512, 1024], P('col', None, 'row'), may hold values from -1.2 to 1.2
- occ_energy: float32 [256], replicated, may hold values from -2 to -0.5
- vir_energy: float32 [512], replicated, may hold values from 0.5 to 3
- block_mask: int32 [256, 8, 16], replicated, may hold values from 0 to 1, as said below
- pair_list: int32 [256, 4], P('col'), may hold values from -1 to 3, as said below
Outputs:
- response_density: float32 [256, 512, 1024], P('col', None, 'row')
- virtual_density: float32 [512, 512], replicated
The draws below stay inside these ranges and needn't reach their ends.
Inputs may be any that keep to these rules, and one draw needn't show every extreme that they name: `block_mask`: each orbital keeps between 32 and 64 of its 128 blocks; some orbital keeps exactly 64. `pair_list`: in each row the live entries come first and are distinct, then -1; every orbital lists at least one partner class; some orbital lists 4.
All inputs are finite; a program needn't handle non-finite values.
Results may differ from the reference program's by a relative error of at most 0.0003.
Values sent between devices are 32-bit elements; how exact they have to be, the bound alone decides.
A program may use at most 128 MiB of HBM per device.

```python
import jax
import jax.numpy as jnp
from jax import lax

NVIR = 512
NAUX = 1024
BLOCK = 64
PAIRS_DEV = 4
NOCC = 256
GROUP_ROWS = 8
NPANEL = 4
NVB = 8
NAB = 16
NBLK = 128
NNZ = 64


def shuffled_rows(base_key, count_rows, width):
    row_keys = jax.random.split(base_key, count_rows)

    def shuffle_one(row_key):
        return jax.random.permutation(row_key, width)
    return jax.vmap(shuffle_one)(row_keys)


def draw_block_mask(key, part):
    count_key = jax.random.fold_in(key, 11)
    order_key = jax.random.fold_in(key, 12)
    chosen_key = jax.random.fold_in(key, 13)
    counts = jax.random.randint(count_key, (NOCC,), NNZ // 2, NNZ + 1)
    chosen = jax.random.randint(chosen_key, (), 0, NOCC)
    counts = jnp.where(jnp.arange(NOCC) == chosen, NNZ, counts)
    shuffled = shuffled_rows(order_key, NOCC, NBLK)
    ranks = jnp.argsort(shuffled, axis=1)
    kept = (ranks < counts[:, None]).astype(jnp.int32)
    return kept.reshape(NOCC, NVB, NAB)


def draw_pair_list(key, part):
    count_key = jax.random.fold_in(key, 21)
    order_key = jax.random.fold_in(key, 22)
    chosen_key = jax.random.fold_in(key, 23)
    counts = jax.random.randint(count_key, (NOCC,), 1, PAIRS_DEV + 1)
    chosen = jax.random.randint(chosen_key, (), 0, NOCC)
    counts = jnp.where(jnp.arange(NOCC) == chosen, PAIRS_DEV, counts)
    shuffled = shuffled_rows(order_key, NOCC, NPANEL)[:, :PAIRS_DEV]
    slots = jnp.arange(PAIRS_DEV)[None, :]
    return jnp.where(slots < counts[:, None], shuffled, -1).astype(jnp.int32)


def steps_of(key, extent, cuts, low, largest):
    gain, own = 1.0, jax.random.fold_in(key, 6)
    for position, blocks in cuts:
        heights = jnp.exp(jax.random.uniform(jax.random.fold_in(own, position), (blocks,), jnp.float32, low / len(cuts), largest / len(cuts)))
        gain = gain * jnp.repeat(heights, extent[position] // blocks).reshape([-1 if axis == position else 1 for axis in range(len(extent))])
    return gain


def scatter_about(rng, extent, scale, bound, shards=(), kind=jnp.bfloat16):
    drawn = jax.random.normal(rng, extent, jnp.float32) * scale
    if len(shards) > 0:
        drawn = steps_of(rng, extent, shards, -0.22, 0.18) * drawn
    return jnp.clip(drawn, min=-bound, max=bound).astype(kind)


def setup_inputs(seed: int = 0) -> dict:
    key_list = jax.random.split(jax.random.key(seed), 6)
    three_index = scatter_about(key_list[0], (NOCC, NVIR, NAUX), 0.15, 1.2, ((0, 32), (2, 8)), jnp.float32)
    occ_energy = jnp.clip(jax.random.uniform(key_list[1], (NOCC,), jnp.float32, -2.0, -0.5), -2.0, -0.5)
    vir_energy = jnp.clip(jax.random.uniform(key_list[2], (NVIR,), jnp.float32, 0.5, 3.0), 0.5, 3.0)
    block_mask = draw_block_mask(jax.random.fold_in(key_list[5], 71), 0)
    pair_list = draw_pair_list(jax.random.fold_in(key_list[5], 71), 0)
    return {"three_index": three_index, "occ_energy": occ_energy, "vir_energy": vir_energy, "block_mask": block_mask, "pair_list": pair_list}


def expand_mask(block_rows):
    widened = jnp.repeat(block_rows.astype(jnp.float32), BLOCK, axis=-2)
    return jnp.repeat(widened, BLOCK, axis=-1)


def pair_terms(own_rows, partner, energy_own, energy_partner, virtual):
    cross_term = lax.dot_general(own_rows, partner, (((1,), (1,)), ((), ())), precision=lax.Precision.HIGHEST, preferred_element_type=jnp.float32)
    denominator = energy_own + energy_partner - virtual[:, None] - virtual[None, :]
    amplitude = cross_term / denominator
    weighted = 2.0 * amplitude - amplitude.T
    response = jnp.dot(weighted, partner, precision=lax.Precision.HIGHEST, preferred_element_type=jnp.float32)
    virt_density = lax.dot_general(weighted, amplitude, (((1,), (1,)), ((), ())), precision=lax.Precision.HIGHEST, preferred_element_type=jnp.float32)
    return response, virt_density


def reference(three_index, occ_energy, vir_energy, block_mask, pair_list):
    masked = three_index * expand_mask(block_mask)

    def one_orbital(density_sum, orbital):
        own_rows = masked[orbital]
        residue = orbital % GROUP_ROWS
        response_sum = jnp.zeros((NVIR, NAUX), jnp.float32)
        for slot_index in range(PAIRS_DEV):
            listed = pair_list[orbital, slot_index]
            live = (listed >= 0).astype(jnp.float32)
            partner_orbital = (jnp.maximum(listed, 0) * GROUP_ROWS + residue).astype(jnp.int32)
            response, virt_density = pair_terms(own_rows, masked[partner_orbital], occ_energy[orbital], occ_energy[partner_orbital], vir_energy)
            response_sum = response_sum + live * response
            density_sum = density_sum + live * virt_density
        return density_sum, response_sum

    density_sum, responses = lax.scan(one_orbital, jnp.zeros((NVIR, NVIR), jnp.float32), jnp.arange(NOCC, dtype=jnp.int32))
    return responses, density_sum / NOCC
```

```python
import jax
import jax.numpy as jnp
from jax import lax
from jax.experimental import pallas as pl
from jax.experimental.pallas import tpu as pltpu
from jax.sharding import PartitionSpec as P

NVIR = 512
NAUX = 1024
BLOCK = 64
PAIRS_DEV = 4
NPANEL = 4
ROWS = 8
WIDTH = NAUX // ROWS
CHUNKS = 2
PIECE = NVIR // CHUNKS
STEPS = ROWS * CHUNKS
MESH = pl.DeviceIdType.MESH
F32 = jnp.float32
BF16 = jnp.bfloat16


def dot_nt(a, b):
    return lax.dot_general(a, b, (((1,), (1,)), ((), ())), preferred_element_type=F32)


def dot_nn(a, b):
    return lax.dot_general(a, b, (((1,), (0,)), ((), ())), preferred_element_type=F32)


def split(x):
    high = x.astype(BF16)
    return high, (x - high.astype(F32)).astype(BF16)


def slice_offset(t):
    return jnp.where(t % 2 == 1, (t + 1) // 2, ROWS - t // 2)


def kernel(
    x_ref, occ_ref, virc_ref, virr_ref, mask_ref, pair_ref,
    resp_ref, dens_ref,
    buf, mbuf, maskx, oh, ol, ph, pw, acc, recip, ah, al, wh, wl, rbuf,
    d1, d1r, d2, d2r, d3, d3r, d4, d4r, g,
    zs, zr, xs1, xs2, xr1, xr2, ys1, yr1, ys2, yr2, cs1, cr1, cs2, cr2,
    rs, rr, ds, dr, loc,
):
    r = lax.axis_index("row")
    c = lax.axis_index("col")
    x, y, k = c // 8, (c // 2) % 4, c % 2

    def col(xx, yy, kk):
        return (xx * 4 + yy) * 2 + kk

    own = jnp.where(c < NPANEL, c, NPANEL)
    first = k + 2 * jnp.where((y == 1) | (y == 2), 1, 0)
    second = k + 2 - 2 * jnp.where((y == 1) | (y == 2), 1, 0)
    y1, y2 = y + 1 - 2 * (y % 2), 3 - y

    def remote(src, dst, ssem, rsem, row, column):
        return pltpu.make_async_remote_copy(
            src_ref=src, dst_ref=dst, send_sem=ssem, recv_sem=rsem,
            device_id=(row, column), device_id_type=MESH,
        )

    barrier = pltpu.get_barrier_semaphore()
    for d in range(1, ROWS):
        pl.semaphore_signal(barrier, inc=1, device_id=((r + d) % ROWS, c), device_id_type=MESH)
    for d in range(1, 4):
        pl.semaphore_signal(barrier, inc=1, device_id=(r, col((x + d) % 4, y, k)), device_id_type=MESH)
        pl.semaphore_signal(barrier, inc=1, device_id=(r, col(x, (y + d) % 4, k)), device_id_type=MESH)
    pl.semaphore_signal(barrier, inc=1, device_id=(r, col(x, y, 1 - k)), device_id_type=MESH)

    local = pltpu.make_async_copy(x_ref.at[r], buf.at[own, 0], loc.at[0])
    local.start()
    for p in range(NPANEL):
        pltpu.make_async_copy(mask_ref.at[ROWS * p + r], mbuf.at[p], loc.at[1 + p]).start()
    pltpu.make_async_copy(mask_ref.at[ROWS * c + r], mbuf.at[NPANEL], loc.at[1 + NPANEL]).start()
    pl.semaphore_wait(barrier, 14)

    def z_copy(t, ch):
        rows = pl.ds(ch * PIECE, PIECE)
        peer = (r + slice_offset(t)) % ROWS
        i = t * CHUNKS + ch
        return remote(x_ref.at[peer, rows], buf.at[own, t, rows], zs.at[i], zr.at[i], peer, c)

    @pl.loop(CHUNKS, STEPS)
    def _(i):
        z_copy(i // CHUNKS, i % CHUNKS).start()

    def piece(q, i):
        return buf.at[q, i // CHUNKS, pl.ds((i % CHUNKS) * PIECE, PIECE)]

    def half(q, i, h):
        return buf.at[q, i // CHUNKS, pl.ds((i % CHUNKS) * PIECE + h * (PIECE // 2), PIECE // 2)]

    def x_out(i, to, ssem):
        return remote(piece(first, i), piece(first, i), ssem.at[i], xr1.at[i], r, col(to, y, k))

    def x_half(i, h):
        return remote(half(first, i, h), half(first, i, h), xs1.at[i], xr2.at[i, h], r, col(2, y, k))

    def y_one(q, i):
        return remote(piece(q, i), piece(q, i), ys1.at[i], yr1.at[i], r, col(x, y1, k))

    def y_two(q, i):
        return remote(piece(q, i), piece(q, i), ys2.at[i], yr2.at[i], r, col(x, y2, k))

    def core(q, i, ssem, rsem):
        return remote(piece(q, i), piece(q, i), ssem.at[i], rsem.at[i], r, col(x, y, 1 - k))

    def wait_z(i):
        @pl.when(i >= CHUNKS)
        def _():
            z_copy(i // CHUNKS, i % CHUNKS).wait_recv()

    def send_first(i):
        @pl.when(y < 2)
        def _():
            @pl.when(x == 0)
            def _():
                wait_z(i)
                x_out(i, 1, xs1).start()
                x_out(i, 3, xs2).start()

            @pl.when(x == 1)
            def _():
                x_out(i, 1, xs1).wait_recv()
                x_half(i, 0).start()

            @pl.when(x == 3)
            def _():
                x_out(i, 3, xs1).wait_recv()
                x_half(i, 1).start()

            @pl.when(x == 2)
            def _():
                x_half(i, 0).wait_recv()
                x_half(i, 1).wait_recv()

            y_two(first, i).start()

        @pl.when(y >= 2)
        def _():
            y_two(first, i).wait_recv()

        y_one(first, i).start()
        core(first, i, cs1, cr1).start()

    def send_second(i):
        y_one(second, i).wait_recv()
        core(second, i, cs2, cr2).start()

    def arrived(i):
        core(first + 1 - 2 * k, i, cs1, cr1).wait_recv()
        core(second + 1 - 2 * k, i, cs2, cr2).wait_recv()

    for n in range(NPANEL + 1):
        orbital = ROWS * (n if n < NPANEL else c) + r
        pltpu.make_async_copy(mask_ref.at[orbital], mbuf.at[n], loc.at[1 + n]).wait()
    masks = jnp.concatenate([mbuf[n] for n in range(NPANEL + 1)], axis=0).astype(F32).astype(BF16)
    for t in range(ROWS):
        s = (r - slice_offset(t) + ROWS) % ROWS
        block = lax.broadcasted_iota(jnp.int32, (2 * ROWS, WIDTH), 0)
        lane = lax.broadcasted_iota(jnp.int32, (2 * ROWS, WIDTH), 1)
        chosen = (block == 2 * s + lane // BLOCK).astype(F32).astype(BF16)
        wide = dot_nn(masks, chosen)
        for n in range(NPANEL + 1):
            maskx[t, n] = wide[n * 8:(n + 1) * 8]

    local.wait()

    def set_recip(p):
        pair = occ_ref[ROWS * c + r] + occ_ref[ROWS * p + r]
        live = jnp.float32(0.0)
        for s in range(PAIRS_DEV):
            live = jnp.where(pair_ref[r, s] == p, jnp.float32(1.0), live)
        for a in range(0, NVIR, 128):
            recip[p, a:a + 128] = live / (pair - virc_ref[a:a + 128] - virr_ref[...])

    def convert(j):
        def one(q, index, hi_ref, lo_ref):
            for h in range(2):
                t = 2 * j + h
                rows = maskx[t, index]
                for b in range(NVIR // BLOCK):
                    a = slice(b * BLOCK, (b + 1) * BLOCK)
                    high, low = split(buf[q, t, a, :] * rows[b:b + 1, :])
                    hi_ref[a, h * WIDTH:(h + 1) * WIDTH] = high
                    lo_ref[a, h * WIDTH:(h + 1) * WIDTH] = low

        one(own, NPANEL, oh.at[j], ol.at[j])

        @pl.loop(0, NPANEL)
        def _(p):
            one(p, p, ph.at[j, p], pw.at[j, p])

    def cross(j):
        @pl.loop(0, NPANEL)
        def _(p):
            term = dot_nt(oh[j], ph[j, p]) + dot_nt(oh[j], pw[j, p]) + dot_nt(ol[j], ph[j, p])

            @pl.when(j == 0)
            def _():
                acc[p] = term

            @pl.when(j > 0)
            def _():
                acc[p] += term

    send_first(0)

    @pl.loop(0, NPANEL)
    def _(j):
        @pl.loop(0, 2 * CHUNKS)
        def _(n):
            i = j * 2 * CHUNKS + n

            @pl.when(i + 1 < STEPS)
            def _():
                send_first(i + 1)

            send_second(i)

        set_recip(j)

        @pl.loop(0, 2 * CHUNKS)
        def _(n):
            i = j * 2 * CHUNKS + n

            @pl.when(jnp.logical_not((x == 0) & (y < 2)))
            def _():
                wait_z(i)

            arrived(i)

        convert(j)
        cross(j)

    @pl.loop(0, NPANEL)
    def _(p):
        for a in range(0, NVIR, 128):
            rows = slice(a, a + 128)
            here = acc[p, rows, :]
            turned = acc[p, :, rows].T
            scale = recip[p, rows, :]
            amplitude = here * scale
            high, low = split(amplitude)
            ah[p, rows, :] = high
            al[p, rows, :] = low
            high, low = split(2.0 * amplitude - turned * scale)
            wh[p, rows, :] = high
            wl[p, rows, :] = low

    def r_copy(t):
        peer = (r - slice_offset(t) + ROWS) % ROWS
        return remote(rbuf.at[t], resp_ref.at[r], rs.at[t], rr.at[t], peer, c)

    def response(j):
        total = None
        for p in range(NPANEL):
            term = dot_nn(wh[p], ph[j, p]) + dot_nn(wh[p], pw[j, p]) + dot_nn(wl[p], ph[j, p])
            total = term if total is None else total + term
        rbuf[2 * j] = total[:, :WIDTH]
        rbuf[2 * j + 1] = total[:, WIDTH:]

        @pl.when(j > 0)
        def _():
            r_copy(2 * j).start()

        r_copy(2 * j + 1).start()

    def r_arrival(t):
        peer = (r + slice_offset(t)) % ROWS
        return remote(rbuf.at[t], resp_ref.at[peer], rs.at[t], rr.at[t], peer, c)

    def d_copy(src, dst, n, row, column):
        return remote(src, dst, ds.at[n], dr.at[n], row, column)

    half_rows = NVIR // 2

    def stage1():
        return d_copy(d1.at[pl.ds((1 - k) * half_rows, half_rows)], d1r, 0, r, col(x, y, 1 - k))

    def stage2(d):
        to = (y + d) % 4
        return d_copy(d2.at[pl.ds(to * 64, 64)], d2r.at[d - 1], d, r, col(x, to, k))

    def stage3(d):
        to = (x + d) % 4
        return d_copy(d3.at[pl.ds(to * 16, 16)], d3r.at[d - 1], 3 + d, r, col(to, y, k))

    def tile(ref, base, row):
        return ref.at[pl.ds(base + (row // 4) * 8, 8), pl.ds((row % 4) * 128, 128)]

    def stage4(d):
        to = (r + d) % ROWS
        return d_copy(tile(d4, 0, to), d4r.at[d - 1], 6 + d, to, c)

    base3 = k * 256 + y * 64 + x * 16
    base2 = k * 256 + y * 64
    base1 = k * 256

    def back4(d, arriving=False):
        to = (r + d) % ROWS
        where = tile(g, base3, (r - d + ROWS) % ROWS if arriving else r)
        return d_copy(where, where, 13 + d, to, c)

    def back3(d, arriving=False):
        source = (x - d + 4) % 4 if arriving else x
        where = g.at[pl.ds(base2 + source * 16, 16)]
        return d_copy(where, where, 20 + d, r, col((x + d) % 4, y, k))

    def back2(d, arriving=False):
        source = (y - d + 4) % 4 if arriving else y
        where = g.at[pl.ds(base1 + source * 64, 64)]
        return d_copy(where, where, 23 + d, r, col(x, (y + d) % 4, k))

    def back1(arriving=False):
        where = g.at[pl.ds((1 - k if arriving else k) * 256, 256)]
        return d_copy(where, where, 27, r, col(x, y, 1 - k))

    response(0)

    @pl.loop(0, NPANEL)
    def _(p):
        term = dot_nt(wh[p], ah[p]) + dot_nt(wh[p], al[p]) + dot_nt(wl[p], ah[p])

        @pl.when(p == 0)
        def _():
            d1[...] = term

        @pl.when(p > 0)
        def _():
            d1[...] += term

    keep = pltpu.make_async_copy(rbuf.at[0], resp_ref.at[r], loc.at[0])
    keep.start()
    stage1().start()
    response(1)
    stage1().wait_recv()
    d2[...] = d1[pl.ds(k * half_rows, half_rows), :] + d1r[...]
    for d in range(1, 4):
        stage2(d).start()
    response(2)
    for d in range(1, 4):
        stage2(d).wait_recv()
    d3[...] = d2[pl.ds(y * 64, 64), :] + d2r[0] + d2r[1] + d2r[2]
    for d in range(1, 4):
        stage3(d).start()
    for d in range(1, 4):
        stage3(d).wait_recv()
    d4[...] = d3[pl.ds(x * 16, 16), :] + d3r[0] + d3r[1] + d3r[2]
    for d in range(1, ROWS):
        stage4(d).start()
    response(3)
    for d in range(1, ROWS):
        stage4(d).wait_recv()
    mine = d4[pl.ds((r // 4) * 8, 8), pl.ds((r % 4) * 128, 128)]
    for d in range(1, ROWS):
        mine = mine + d4r[d - 1]
    g[pl.ds(base3 + (r // 4) * 8, 8), pl.ds((r % 4) * 128, 128)] = mine * (1.0 / 256.0)
    for d in range(1, ROWS):
        back4(d).start()
    for d in range(1, ROWS):
        back4(d, True).wait_recv()
    for d in range(1, 4):
        back3(d).start()
    for d in range(1, 4):
        back3(d, True).wait_recv()
    for d in range(1, 4):
        back2(d).start()
    for d in range(1, 4):
        back2(d, True).wait_recv()
    back1().start()
    back1(True).wait_recv()
    out = pltpu.make_async_copy(g, dens_ref, loc.at[1])
    out.start()

    keep.wait()
    for t in range(1, ROWS):
        r_arrival(t).wait_recv()
    out.wait()
    for t in range(1, ROWS):
        r_copy(t).wait_send()
    stage1().wait_send()
    back1().wait_send()
    for d in range(1, 4):
        stage2(d).wait_send()
        stage3(d).wait_send()
        back3(d).wait_send()
        back2(d).wait_send()
    for d in range(1, ROWS):
        stage4(d).wait_send()
        back4(d).wait_send()

    @pl.loop(0, STEPS)
    def _(i):
        @pl.when(i >= CHUNKS)
        def _():
            z_copy(i // CHUNKS, i % CHUNKS).wait_send()

        @pl.when(y < 2)
        def _():
            @pl.when(x == 0)
            def _():
                x_out(i, 1, xs1).wait_send()
                x_out(i, 3, xs2).wait_send()

            @pl.when((x == 1) | (x == 3))
            def _():
                x_half(i, x // 2).wait_send()

            y_two(first, i).wait_send()

        y_one(first, i).wait_send()
        core(first, i, cs1, cr1).wait_send()
        core(second, i, cs2, cr2).wait_send()


def on_device(three_index, occ_energy, vir_energy, block_mask, pair_list):
    any_space = pl.BlockSpec(memory_space=pl.ANY)
    vmem = pl.BlockSpec(memory_space=pltpu.VMEM)
    smem = pl.BlockSpec(memory_space=pltpu.SMEM)
    dma = pltpu.SemaphoreType.DMA
    square = (NPANEL, NVIR, NVIR)
    return pl.pallas_call(
        kernel,
        out_shape=(
            jax.ShapeDtypeStruct((ROWS, NVIR, WIDTH), F32),
            jax.ShapeDtypeStruct((NVIR, NVIR), F32),
        ),
        in_specs=[any_space, smem, vmem, vmem, any_space, smem],
        out_specs=(any_space, any_space),
        scratch_shapes=[
            pltpu.VMEM((NPANEL + 1, ROWS, NVIR, WIDTH), F32),
            pltpu.VMEM((NPANEL + 1, 8, 16), jnp.int32),
            pltpu.VMEM((ROWS, NPANEL + 1, 8, WIDTH), F32),
            pltpu.VMEM((4, NVIR, 2 * WIDTH), BF16),
            pltpu.VMEM((4, NVIR, 2 * WIDTH), BF16),
            pltpu.VMEM((4, NPANEL, NVIR, 2 * WIDTH), BF16),
            pltpu.VMEM((4, NPANEL, NVIR, 2 * WIDTH), BF16),
            pltpu.VMEM(square, F32),
            pltpu.VMEM(square, F32),
            pltpu.VMEM(square, BF16),
            pltpu.VMEM(square, BF16),
            pltpu.VMEM(square, BF16),
            pltpu.VMEM(square, BF16),
            pltpu.VMEM((ROWS, NVIR, WIDTH), F32),
            pltpu.VMEM((512, NVIR), F32),
            pltpu.VMEM((256, NVIR), F32),
            pltpu.VMEM((256, NVIR), F32),
            pltpu.VMEM((3, 64, NVIR), F32),
            pltpu.VMEM((64, NVIR), F32),
            pltpu.VMEM((3, 16, NVIR), F32),
            pltpu.VMEM((16, NVIR), F32),
            pltpu.VMEM((7, 8, 128), F32),
            pltpu.VMEM((NVIR, NVIR), F32),
            dma((STEPS,)), dma((STEPS,)),
            dma((STEPS,)), dma((STEPS,)), dma((STEPS,)), dma((STEPS, 2)),
            dma((STEPS,)), dma((STEPS,)), dma((STEPS,)), dma((STEPS,)),
            dma((STEPS,)), dma((STEPS,)), dma((STEPS,)), dma((STEPS,)),
            dma((ROWS,)), dma((ROWS,)), dma((28,)), dma((28,)), dma((6,)),
        ],
        compiler_params=pltpu.CompilerParams(
            collective_id=0, has_side_effects=True, vmem_limit_bytes=62 * 1024 * 1024
        ),
    )(
        three_index, occ_energy, vir_energy[:, None], vir_energy[None, :], block_mask, pair_list
    )


def solution(mesh):
    placed = (P("col", None, "row"), P(), P(), P(), P("col", None))
    return jax.shard_map(
        on_device,
        mesh=mesh,
        in_specs=placed,
        out_specs=(P("col", None, "row"), P()),
        check_vma=False,
    )
```

```python
import jax
import jax.numpy as jnp
from jax import lax
from jax.experimental import pallas as pl
from jax.experimental.pallas import tpu as pltpu
from jax.sharding import PartitionSpec as P

NVIR = 512
NAUX = 1024
BLOCK = 64
PAIRS_DEV = 4
NPANEL = 4
ROWS = 8
COLS = 32
WIDTH = NAUX // ROWS
CHUNKS = 2
PIECE = NVIR // CHUNKS
STEPS = ROWS * CHUNKS
VMEM_LIMIT = 46 * 1024 * 1024
MESH = pl.DeviceIdType.MESH
F32 = jnp.float32
BF16 = jnp.bfloat16


def dot_nt(a, b):
    return lax.dot_general(a, b, (((1,), (1,)), ((), ())), preferred_element_type=F32)


def dot_nn(a, b):
    return lax.dot_general(a, b, (((1,), (0,)), ((), ())), preferred_element_type=F32)


def split(x):
    high = x.astype(BF16)
    return high, (x - high.astype(F32)).astype(BF16)


def slice_offset(t):
    return jnp.where(t % 2 == 1, (t + 1) // 2, ROWS - t // 2)


def kernel(
    x_ref, occ_ref, vir_ref, mask_ref, pair_ref,
    resp_ref, dens_ref,
    buf, mbuf, maskx, vcol, oh, ol, ph, pw, acc, recip, ah, al, wh, wl, rbuf,
    d1, d1r, d2, d2r, d3, d3r, d4, d4r, g,
    zs, zr, xs1, xs2, xr1, xr2, ys1, yr1, ys2, yr2, cs1, cr1, cs2, cr2,
    rs, rr, ds, dr, loc,
):
    r = lax.axis_index("row")
    c = lax.axis_index("col")
    x, y, k = c // 8, (c // 2) % 4, c % 2

    def col(xx, yy, kk):
        return (xx * 4 + yy) * 2 + kk

    own = jnp.where(c < NPANEL, c, NPANEL)
    first = k + 2 * jnp.where((y == 1) | (y == 2), 1, 0)
    second = k + 2 - 2 * jnp.where((y == 1) | (y == 2), 1, 0)
    y1, y2 = y + 1 - 2 * (y % 2), 3 - y

    half_rows = NVIR // 2

    def remote(src, dst, ssem, rsem, row, column):
        return pltpu.make_async_remote_copy(
            src_ref=src, dst_ref=dst, send_sem=ssem, recv_sem=rsem,
            device_id=(row, column), device_id_type=MESH,
        )

    barrier = pltpu.get_barrier_semaphore()
    for d in range(1, ROWS):
        pl.semaphore_signal(barrier, inc=1, device_id=((r + d) % ROWS, c), device_id_type=MESH)
    for d in range(1, 4):
        pl.semaphore_signal(barrier, inc=1, device_id=(r, col((x + d) % 4, y, k)), device_id_type=MESH)
        pl.semaphore_signal(barrier, inc=1, device_id=(r, col(x, (y + d) % 4, k)), device_id_type=MESH)
    pl.semaphore_signal(barrier, inc=1, device_id=(r, col(x, y, 1 - k)), device_id_type=MESH)

    local = pltpu.make_async_copy(x_ref.at[r], buf.at[own, 0], loc.at[0])
    local.start()
    mask_copy = pltpu.make_async_copy(mask_ref, mbuf, loc.at[1])
    mask_copy.start()
    pl.semaphore_wait(barrier, 14)

    def z_copy(t, ch):
        rows = pl.ds(ch * PIECE, PIECE)
        peer = (r + slice_offset(t)) % ROWS
        i = t * CHUNKS + ch
        return remote(x_ref.at[peer, rows], buf.at[own, t, rows], zs.at[i], zr.at[i], peer, c)

    @pl.loop(CHUNKS, STEPS)
    def _(i):
        z_copy(i // CHUNKS, i % CHUNKS).start()

    def piece(q, i):
        return buf.at[q, i // CHUNKS, pl.ds((i % CHUNKS) * PIECE, PIECE)]

    def half(q, i, h):
        return buf.at[q, i // CHUNKS, pl.ds((i % CHUNKS) * PIECE + h * (PIECE // 2), PIECE // 2)]

    def x_out(i, to, ssem):
        return remote(piece(first, i), piece(first, i), ssem.at[i], xr1.at[i], r, col(to, y, k))

    def x_half(i, h):
        return remote(half(first, i, h), half(first, i, h), xs1.at[i], xr2.at[i, h], r, col(2, y, k))

    def y_one(q, i):
        return remote(piece(q, i), piece(q, i), ys1.at[i], yr1.at[i], r, col(x, y1, k))

    def y_two(q, i):
        return remote(piece(q, i), piece(q, i), ys2.at[i], yr2.at[i], r, col(x, y2, k))

    def core(q, i, ssem, rsem):
        return remote(piece(q, i), piece(q, i), ssem.at[i], rsem.at[i], r, col(x, y, 1 - k))

    def wait_z(i):
        @pl.when(i >= CHUNKS)
        def _():
            z_copy(i // CHUNKS, i % CHUNKS).wait_recv()

    def send_first(i):
        @pl.when(y < 2)
        def _():
            @pl.when(x == 0)
            def _():
                wait_z(i)
                x_out(i, 1, xs1).start()
                x_out(i, 3, xs2).start()

            @pl.when(x == 1)
            def _():
                x_out(i, 1, xs1).wait_recv()
                x_half(i, 0).start()

            @pl.when(x == 3)
            def _():
                x_out(i, 3, xs1).wait_recv()
                x_half(i, 1).start()

            @pl.when(x == 2)
            def _():
                x_half(i, 0).wait_recv()
                x_half(i, 1).wait_recv()

            y_two(first, i).start()

        @pl.when(y >= 2)
        def _():
            y_two(first, i).wait_recv()

        y_one(first, i).start()
        core(first, i, cs1, cr1).start()

    def send_second(i):
        y_one(second, i).wait_recv()
        core(second, i, cs2, cr2).start()

    def arrived(i):
        core(first + 1 - 2 * k, i, cs1, cr1).wait_recv()
        core(second + 1 - 2 * k, i, cs2, cr2).wait_recv()

    local.wait()
    send_first(0)

    mask_copy.wait()
    flat = mbuf[...].reshape(ROWS * 2 * ROWS, ROWS * COLS).astype(F32).astype(BF16)
    index = lax.broadcasted_iota(jnp.int32, (8, ROWS * COLS), 0)
    orbital = lax.broadcasted_iota(jnp.int32, (8, ROWS * COLS), 1)
    wanted = ROWS * jnp.where(index < NPANEL, index, c) + r
    picked = dot_nt((orbital == wanted).astype(F32).astype(BF16), flat)
    block_of = lax.broadcasted_iota(jnp.int32, (8, 128), 1) >> 4
    band = lax.broadcasted_iota(jnp.int32, (8, 128), 0)
    masks = jnp.concatenate(
        [jnp.where(block_of == band, picked[n:n + 1, :], 0.0) for n in range(NPANEL + 1)], axis=0
    ).astype(BF16)
    block = lax.broadcasted_iota(jnp.int32, (128, WIDTH), 0) & 15
    lane = lax.broadcasted_iota(jnp.int32, (128, WIDTH), 1) >> 6
    for t in range(ROWS):
        s = (r - slice_offset(t) + ROWS) % ROWS
        wide = dot_nn(masks, (block == 2 * s + lane).astype(F32).astype(BF16))
        for n in range(NPANEL + 1):
            maskx[t, n] = wide[n * 8:(n + 1) * 8]
    for a in range(0, NVIR, 128):
        vcol[a:a + 128, :] = jnp.broadcast_to(vir_ref[:, a:a + 128], (128, 128)).T

    def set_recip(p):
        pair = occ_ref[ROWS * c + r] + occ_ref[ROWS * p + r]
        live = jnp.float32(0.0)
        for s in range(PAIRS_DEV):
            live = jnp.where(pair_ref[s, r] == p, jnp.float32(1.0), live)
        for a in range(0, NVIR, 128):
            for b in range(0, NVIR, 128):
                recip[p, a:a + 128, b:b + 128] = live / (
                    pair - vcol[a:a + 128, :] - vir_ref[:, b:b + 128]
                )

    def convert(j, q, index, hi_ref, lo_ref):
        for h in range(2):
            t = 2 * j + h
            rows = maskx[t, index]
            for b in range(NVIR // BLOCK):
                a = slice(b * BLOCK, (b + 1) * BLOCK)
                high, low = split(buf[q, t, a, :] * rows[b:b + 1, :])
                hi_ref[a, h * WIDTH:(h + 1) * WIDTH] = high
                lo_ref[a, h * WIDTH:(h + 1) * WIDTH] = low

    def cross(j, p):
        convert(j, p, p, ph.at[j, p], pw.at[j, p])
        term = dot_nt(oh[j], ph[j, p]) + dot_nt(oh[j], pw[j, p]) + dot_nt(ol[j], ph[j, p])

        @pl.when(j == 0)
        def _():
            acc[p] = term

        @pl.when(j > 0)
        def _():
            acc[p] += term

    def pair_arrived(j):
        @pl.loop(0, 2 * CHUNKS)
        def _(n):
            i = j * 2 * CHUNKS + n

            @pl.when(jnp.logical_not((x == 0) & (y < 2)))
            def _():
                wait_z(i)

            arrived(i)

        convert(j, own, NPANEL, oh.at[j], ol.at[j])

    @pl.loop(0, NPANEL + 1)
    def _(j):
        @pl.when(j < NPANEL)
        def _():
            set_recip(j)

        @pl.loop(0, 4)
        def _(n):
            @pl.when(j < NPANEL)
            def _():
                for m in range(CHUNKS // 2):
                    i = (j * 4 + n) * (CHUNKS // 2) + m

                    @pl.when(i + 1 < STEPS)
                    def _():
                        send_first(i + 1)

                    send_second(i)

            @pl.when(j > 0)
            def _():
                @pl.when(n == 0)
                def _():
                    pair_arrived(j - 1)

                cross(j - 1, n)

    @pl.loop(0, NPANEL)
    def _(p):
        for a in range(0, NVIR, 128):
            rows = slice(a, a + 128)
            here = acc[p, rows, :]
            turned = acc[p, :, rows].T
            scale = recip[p, rows, :]
            amplitude = here * scale
            high, low = split(amplitude)
            ah[p, rows, :] = high
            al[p, rows, :] = low
            high, low = split(2.0 * amplitude - turned * scale)
            wh[p, rows, :] = high
            wl[p, rows, :] = low

    def r_copy(t, h):
        peer = (r - slice_offset(t) + ROWS) % ROWS
        rows = pl.ds(h * half_rows, half_rows)
        i = 2 * t + h
        return remote(rbuf.at[t, rows], resp_ref.at[r, rows], rs.at[i], rr.at[i], peer, c)

    def r_send(t):
        for h in range(2):
            r_copy(t, h).start()

    def response(j):
        total = None
        for p in range(NPANEL):
            term = dot_nn(wh[p], ph[j, p]) + dot_nn(wh[p], pw[j, p]) + dot_nn(wl[p], ph[j, p])
            total = term if total is None else total + term
        rbuf[2 * j] = total[:, :WIDTH]
        rbuf[2 * j + 1] = total[:, WIDTH:]

    def r_arrival(t, h):
        peer = (r + slice_offset(t)) % ROWS
        rows = pl.ds(h * half_rows, half_rows)
        i = 2 * t + h
        return remote(rbuf.at[t, rows], resp_ref.at[peer, rows], rs.at[i], rr.at[i], peer, c)

    def d_copy(src, dst, n, row, column):
        return remote(src, dst, ds.at[n], dr.at[n], row, column)

    def stage1():
        return d_copy(d1.at[pl.ds((1 - k) * half_rows, half_rows)], d1r, 0, r, col(x, y, 1 - k))

    def stage2(d):
        to = (y + d) % 4
        return d_copy(d2.at[pl.ds(to * 64, 64)], d2r.at[d - 1], d, r, col(x, to, k))

    def stage3(d):
        to = (x + d) % 4
        return d_copy(d3.at[pl.ds(to * 16, 16)], d3r.at[d - 1], 3 + d, r, col(to, y, k))

    def tile(ref, base, row):
        return ref.at[pl.ds(base + (row // 4) * 8, 8), pl.ds((row % 4) * 128, 128)]

    def stage4(d):
        to = (r + d) % ROWS
        return d_copy(tile(d4, 0, to), d4r.at[d - 1], 6 + d, to, c)

    base3 = k * 256 + y * 64 + x * 16
    base2 = k * 256 + y * 64
    base1 = k * 256

    def back4(d, arriving=False):
        to = (r + d) % ROWS
        where = tile(g, base3, (r - d + ROWS) % ROWS if arriving else r)
        return d_copy(where, where, 13 + d, to, c)

    def back3(d, arriving=False):
        source = (x - d + 4) % 4 if arriving else x
        where = g.at[pl.ds(base2 + source * 16, 16)]
        return d_copy(where, where, 20 + d, r, col((x + d) % 4, y, k))

    def back2(d, arriving=False):
        source = (y - d + 4) % 4 if arriving else y
        where = g.at[pl.ds(base1 + source * 64, 64)]
        return d_copy(where, where, 23 + d, r, col(x, (y + d) % 4, k))

    def back1(arriving=False):
        where = g.at[pl.ds((1 - k if arriving else k) * 256, 256)]
        return d_copy(where, where, 27, r, col(x, y, 1 - k))

    response(1)
    r_send(2)
    r_send(3)

    @pl.loop(0, NPANEL)
    def _(p):
        term = dot_nt(wh[p], ah[p]) + dot_nt(wh[p], al[p]) + dot_nt(wl[p], ah[p])

        @pl.when(p == 0)
        def _():
            d1[...] = term

        @pl.when(p > 0)
        def _():
            d1[...] += term

    stage1().start()
    response(0)
    r_send(1)
    keep = pltpu.make_async_copy(rbuf.at[0], resp_ref.at[r], loc.at[0])
    keep.start()
    stage1().wait_recv()
    d2[...] = d1[pl.ds(k * half_rows, half_rows), :] + d1r[...]
    for d in range(1, 4):
        stage2(d).start()
    response(2)
    r_send(4)
    response(3)
    for d in range(1, 4):
        stage2(d).wait_recv()
    d3[...] = d2[pl.ds(y * 64, 64), :] + d2r[0] + d2r[1] + d2r[2]
    for d in range(1, 4):
        stage3(d).start()
    for d in range(1, 4):
        stage3(d).wait_recv()
    d4[...] = d3[pl.ds(x * 16, 16), :] + d3r[0] + d3r[1] + d3r[2]
    for d in range(1, ROWS):
        stage4(d).start()
    r_copy(5, 0).start()
    r_copy(6, 0).start()
    for d in range(1, ROWS):
        stage4(d).wait_recv()
    mine = d4[pl.ds((r // 4) * 8, 8), pl.ds((r % 4) * 128, 128)]
    for d in range(1, ROWS):
        mine = mine + d4r[d - 1]
    g[pl.ds(base3 + (r // 4) * 8, 8), pl.ds((r % 4) * 128, 128)] = mine * (1.0 / 256.0)
    for d in range(1, ROWS):
        back4(d).start()
    r_send(7)
    r_copy(5, 1).start()
    r_copy(6, 1).start()
    for d in range(1, ROWS):
        back4(d, True).wait_recv()
    for d in range(1, 4):
        back3(d).start()
    for d in range(1, 4):
        back3(d, True).wait_recv()
    for d in range(1, 4):
        back2(d).start()
    for d in range(1, 4):
        back2(d, True).wait_recv()
    back1().start()
    back1(True).wait_recv()
    out = pltpu.make_async_copy(g, dens_ref, loc.at[1])
    out.start()

    keep.wait()
    for t in range(1, ROWS):
        for h in range(2):
            r_arrival(t, h).wait_recv()
    out.wait()
    for t in range(1, ROWS):
        for h in range(2):
            r_copy(t, h).wait_send()
    stage1().wait_send()
    back1().wait_send()
    for d in range(1, 4):
        stage2(d).wait_send()
        stage3(d).wait_send()
        back3(d).wait_send()
        back2(d).wait_send()
    for d in range(1, ROWS):
        stage4(d).wait_send()
        back4(d).wait_send()

    @pl.loop(0, STEPS)
    def _(i):
        @pl.when(i >= CHUNKS)
        def _():
            z_copy(i // CHUNKS, i % CHUNKS).wait_send()

        @pl.when(y < 2)
        def _():
            @pl.when(x == 0)
            def _():
                x_out(i, 1, xs1).wait_send()
                x_out(i, 3, xs2).wait_send()

            @pl.when((x == 1) | (x == 3))
            def _():
                x_half(i, x // 2).wait_send()

            y_two(first, i).wait_send()

        y_one(first, i).wait_send()
        core(first, i, cs1, cr1).wait_send()
        core(second, i, cs2, cr2).wait_send()


def on_device(three_index, occ_energy, vir_energy, block_mask, pair_list):
    any_space = pl.BlockSpec(memory_space=pl.ANY)
    vmem = pl.BlockSpec(memory_space=pltpu.VMEM)
    smem = pl.BlockSpec(memory_space=pltpu.SMEM)
    dma = pltpu.SemaphoreType.DMA
    square = (NPANEL, NVIR, NVIR)
    return pl.pallas_call(
        kernel,
        out_shape=(
            jax.ShapeDtypeStruct((ROWS, NVIR, WIDTH), F32),
            jax.ShapeDtypeStruct((NVIR, NVIR), F32),
        ),
        in_specs=[any_space, smem, vmem, any_space, smem],
        out_specs=(any_space, any_space),
        scratch_shapes=[
            pltpu.VMEM((NPANEL + 1, ROWS, NVIR, WIDTH), F32),
            pltpu.VMEM((8, 16, ROWS * COLS), jnp.int32),
            pltpu.VMEM((ROWS, NPANEL + 1, 8, WIDTH), F32),
            pltpu.VMEM((NVIR, 128), F32),
            pltpu.VMEM((4, NVIR, 2 * WIDTH), BF16),
            pltpu.VMEM((4, NVIR, 2 * WIDTH), BF16),
            pltpu.VMEM((4, NPANEL, NVIR, 2 * WIDTH), BF16),
            pltpu.VMEM((4, NPANEL, NVIR, 2 * WIDTH), BF16),
            pltpu.VMEM(square, F32),
            pltpu.VMEM(square, F32),
            pltpu.VMEM(square, BF16),
            pltpu.VMEM(square, BF16),
            pltpu.VMEM(square, BF16),
            pltpu.VMEM(square, BF16),
            pltpu.VMEM((ROWS, NVIR, WIDTH), F32),
            pltpu.VMEM((512, NVIR), F32),
            pltpu.VMEM((256, NVIR), F32),
            pltpu.VMEM((256, NVIR), F32),
            pltpu.VMEM((3, 64, NVIR), F32),
            pltpu.VMEM((64, NVIR), F32),
            pltpu.VMEM((3, 16, NVIR), F32),
            pltpu.VMEM((16, NVIR), F32),
            pltpu.VMEM((7, 8, 128), F32),
            pltpu.VMEM((NVIR, NVIR), F32),
            dma((STEPS,)), dma((STEPS,)),
            dma((STEPS,)), dma((STEPS,)), dma((STEPS,)), dma((STEPS, 2)),
            dma((STEPS,)), dma((STEPS,)), dma((STEPS,)), dma((STEPS,)),
            dma((STEPS,)), dma((STEPS,)), dma((STEPS,)), dma((STEPS,)),
            dma((2 * ROWS,)), dma((2 * ROWS,)), dma((28,)), dma((28,)), dma((2,)),
        ],
        compiler_params=pltpu.CompilerParams(
            collective_id=0, has_side_effects=True, vmem_limit_bytes=VMEM_LIMIT
        ),
    )(
        three_index, occ_energy, vir_energy[None, :], block_mask.transpose(1, 2, 0), pair_list.T
    )


def solution(mesh):
    placed = (P("col", None, "row"), P(), P(), P(), P("col", None))
    return jax.shard_map(
        on_device,
        mesh=mesh,
        in_specs=placed,
        out_specs=(P("col", None, "row"), P()),
        check_vma=False,
    )
```

```python
import jax
import jax.numpy as jnp
from jax import lax
from jax.experimental import pallas as pl
from jax.experimental.pallas import tpu as pltpu
from jax.sharding import PartitionSpec as P

NVIR = 512
NAUX = 1024
BLOCK = 64
PAIRS_DEV = 4
NPANEL = 4
ROWS = 8
COLS = 32
WIDTH = NAUX // ROWS
CHUNKS = 4
PIECE = NVIR // CHUNKS
STEPS = ROWS * CHUNKS
PER_UNIT = CHUNKS // 2
LAG = 3
BEHIND = (LAG + PER_UNIT - 2) // PER_UNIT
VMEM_LIMIT = 50 * 1024 * 1024
MESH = pl.DeviceIdType.MESH
F32 = jnp.float32
BF16 = jnp.bfloat16


def dot_nt(a, b):
    return lax.dot_general(a, b, (((1,), (1,)), ((), ())), preferred_element_type=F32)


def dot_nn(a, b):
    return lax.dot_general(a, b, (((1,), (0,)), ((), ())), preferred_element_type=F32)


def split(x):
    high = x.astype(BF16)
    return high, (x - high.astype(F32)).astype(BF16)


def slice_offset(t):
    return jnp.where(t % 2 == 1, (t + 1) // 2, ROWS - t // 2)


def kernel(
    x_ref, occ_ref, vir_ref, mask_ref, pair_ref,
    resp_ref, dens_ref,
    buf, mbuf, maskx, vcol, oh, ol, ph, pw, acc, recip, ah, al, wh, wl, rbuf,
    d1, d1r, d2, d2r, d3, d3r, d4, d4r, g,
    zs, zr, xs1, xs2, xr1, xr2, ys1, yr1, ys2, yr2, cs1, cr1, cs2, cr2,
    rs, rr, ds, dr, loc,
):
    r = lax.axis_index("row")
    c = lax.axis_index("col")
    x, y, k = c // 8, (c // 2) % 4, c % 2

    def col(xx, yy, kk):
        return (xx * 4 + yy) * 2 + kk

    own = jnp.where(c < NPANEL, c, NPANEL)
    first = k + 2 * jnp.where((y == 1) | (y == 2), 1, 0)
    second = k + 2 - 2 * jnp.where((y == 1) | (y == 2), 1, 0)
    y1, y2 = y + 1 - 2 * (y % 2), 3 - y

    half_rows = NVIR // 2

    def remote(src, dst, ssem, rsem, row, column):
        return pltpu.make_async_remote_copy(
            src_ref=src, dst_ref=dst, send_sem=ssem, recv_sem=rsem,
            device_id=(row, column), device_id_type=MESH,
        )

    barrier = pltpu.get_barrier_semaphore()
    for d in range(1, ROWS):
        pl.semaphore_signal(barrier, inc=1, device_id=((r + d) % ROWS, c), device_id_type=MESH)
    for d in range(1, 4):
        pl.semaphore_signal(barrier, inc=1, device_id=(r, col((x + d) % 4, y, k)), device_id_type=MESH)
        pl.semaphore_signal(barrier, inc=1, device_id=(r, col(x, (y + d) % 4, k)), device_id_type=MESH)
    pl.semaphore_signal(barrier, inc=1, device_id=(r, col(x, y, 1 - k)), device_id_type=MESH)

    local = pltpu.make_async_copy(x_ref.at[r], buf.at[own, 0], loc.at[0])
    local.start()
    mask_copy = pltpu.make_async_copy(mask_ref, mbuf, loc.at[1])
    mask_copy.start()
    pl.semaphore_wait(barrier, 14)

    def z_copy(t, ch):
        rows = pl.ds(ch * PIECE, PIECE)
        peer = (r + slice_offset(t)) % ROWS
        i = t * CHUNKS + ch
        return remote(x_ref.at[peer, rows], buf.at[own, t, rows], zs.at[i], zr.at[i], peer, c)

    @pl.loop(CHUNKS, STEPS)
    def _(i):
        z_copy(i // CHUNKS, i % CHUNKS).start()

    def piece(q, i):
        return buf.at[q, i // CHUNKS, pl.ds((i % CHUNKS) * PIECE, PIECE)]

    def half(q, i, h):
        return buf.at[q, i // CHUNKS, pl.ds((i % CHUNKS) * PIECE + h * (PIECE // 2), PIECE // 2)]

    def x_out(i, to, ssem):
        return remote(piece(first, i), piece(first, i), ssem.at[i], xr1.at[i], r, col(to, y, k))

    def x_half(i, h):
        return remote(half(first, i, h), half(first, i, h), xs1.at[i], xr2.at[i, h], r, col(2, y, k))

    def y_one(q, i):
        return remote(piece(q, i), piece(q, i), ys1.at[i], yr1.at[i], r, col(x, y1, k))

    def y_two(q, i):
        return remote(piece(q, i), piece(q, i), ys2.at[i], yr2.at[i], r, col(x, y2, k))

    def core(q, i, ssem, rsem):
        return remote(piece(q, i), piece(q, i), ssem.at[i], rsem.at[i], r, col(x, y, 1 - k))

    def wait_z(i):
        @pl.when(i >= CHUNKS)
        def _():
            z_copy(i // CHUNKS, i % CHUNKS).wait_recv()

    def send_first(i):
        @pl.when(y < 2)
        def _():
            @pl.when(x == 0)
            def _():
                wait_z(i)
                x_out(i, 1, xs1).start()
                x_out(i, 3, xs2).start()

            @pl.when(x == 1)
            def _():
                x_out(i, 1, xs1).wait_recv()
                x_half(i, 0).start()

            @pl.when(x == 3)
            def _():
                x_out(i, 3, xs1).wait_recv()
                x_half(i, 1).start()

            @pl.when(x == 2)
            def _():
                x_half(i, 0).wait_recv()
                x_half(i, 1).wait_recv()

            y_two(first, i).start()

        @pl.when(y >= 2)
        def _():
            y_two(first, i).wait_recv()

        y_one(first, i).start()
        core(first, i, cs1, cr1).start()

    def send_second(i):
        y_one(second, i).wait_recv()
        core(second, i, cs2, cr2).start()

    def arrived(i):
        core(first + 1 - 2 * k, i, cs1, cr1).wait_recv()
        core(second + 1 - 2 * k, i, cs2, cr2).wait_recv()

    local.wait()
    send_first(0)

    mask_copy.wait()
    flat = mbuf[...].reshape(ROWS * 2 * ROWS, ROWS * COLS).astype(F32).astype(BF16)
    index = lax.broadcasted_iota(jnp.int32, (8, ROWS * COLS), 0)
    orbital = lax.broadcasted_iota(jnp.int32, (8, ROWS * COLS), 1)
    wanted = ROWS * jnp.where(index < NPANEL, index, c) + r
    picked = dot_nt((orbital == wanted).astype(F32).astype(BF16), flat)
    block_of = lax.broadcasted_iota(jnp.int32, (8, 128), 1) >> 4
    band = lax.broadcasted_iota(jnp.int32, (8, 128), 0)
    masks = jnp.concatenate(
        [jnp.where(block_of == band, picked[n:n + 1, :], 0.0) for n in range(NPANEL + 1)], axis=0
    ).astype(BF16)
    block = lax.broadcasted_iota(jnp.int32, (128, WIDTH), 0) & 15
    lane = lax.broadcasted_iota(jnp.int32, (128, WIDTH), 1) >> 6
    for t in range(ROWS):
        s = (r - slice_offset(t) + ROWS) % ROWS
        wide = dot_nn(masks, (block == 2 * s + lane).astype(F32).astype(BF16))
        for n in range(NPANEL + 1):
            maskx[t, n] = wide[n * 8:(n + 1) * 8]
    for a in range(0, NVIR, 128):
        vcol[a:a + 128, :] = jnp.broadcast_to(vir_ref[:, a:a + 128], (128, 128)).T

    def set_recip(p):
        pair = occ_ref[ROWS * c + r] + occ_ref[ROWS * p + r]
        live = jnp.float32(0.0)
        for s in range(PAIRS_DEV):
            live = jnp.where(pair_ref[s, r] == p, jnp.float32(1.0), live)
        for a in range(0, NVIR, 128):
            for b in range(0, NVIR, 128):
                recip[p, a:a + 128, b:b + 128] = live / (
                    pair - vcol[a:a + 128, :] - vir_ref[:, b:b + 128]
                )

    def convert(j, q, index, hi_ref, lo_ref):
        for h in range(2):
            t = 2 * j + h
            rows = maskx[t, index]
            for b in range(NVIR // BLOCK):
                a = slice(b * BLOCK, (b + 1) * BLOCK)
                high, low = split(buf[q, t, a, :] * rows[b:b + 1, :])
                hi_ref[a, h * WIDTH:(h + 1) * WIDTH] = high
                lo_ref[a, h * WIDTH:(h + 1) * WIDTH] = low

    def cross(j, p):
        convert(j, p, p, ph.at[j, p], pw.at[j, p])
        term = dot_nt(oh[j], ph[j, p]) + dot_nt(oh[j], pw[j, p]) + dot_nt(ol[j], ph[j, p])

        @pl.when(j == 0)
        def _():
            acc[p] = term

        @pl.when(j > 0)
        def _():
            acc[p] += term

    def pair_arrived(j):
        @pl.loop(0, 2 * CHUNKS)
        def _(n):
            i = j * 2 * CHUNKS + n

            @pl.when(jnp.logical_not((x == 0) & (y < 2)))
            def _():
                wait_z(i)

            arrived(i)

        convert(j, own, NPANEL, oh.at[j], ol.at[j])

    @pl.loop(0, 4 * NPANEL + 4 + BEHIND)
    def _(v):
        for m in range(PER_UNIT):
            i = v * PER_UNIT + m

            @pl.when(i + 1 < STEPS)
            def _():
                send_first(i + 1)

            late = i + 1 - LAG

            @pl.when((late >= 0) & (late < STEPS))
            def _():
                send_second(late)

        @pl.when(v < NPANEL)
        def _():
            set_recip(v)

        unit = v - 4 - BEHIND

        @pl.when((unit >= 0) & (unit < 4 * NPANEL))
        def _():
            @pl.when(unit % 4 == 0)
            def _():
                pair_arrived(unit // 4)

            cross(unit // 4, unit % 4)

    @pl.loop(0, NPANEL)
    def _(p):
        for a in range(0, NVIR, 128):
            rows = slice(a, a + 128)
            here = acc[p, rows, :]
            turned = acc[p, :, rows].T
            scale = recip[p, rows, :]
            amplitude = here * scale
            high, low = split(amplitude)
            ah[p, rows, :] = high
            al[p, rows, :] = low
            high, low = split(2.0 * amplitude - turned * scale)
            wh[p, rows, :] = high
            wl[p, rows, :] = low

    def r_copy(t, h):
        peer = (r - slice_offset(t) + ROWS) % ROWS
        rows = pl.ds(h * half_rows, half_rows)
        i = 2 * t + h
        return remote(rbuf.at[t, rows], resp_ref.at[r, rows], rs.at[i], rr.at[i], peer, c)

    def r_send(t):
        for h in range(2):
            r_copy(t, h).start()

    def response(j):
        total = None
        for p in range(NPANEL):
            term = dot_nn(wh[p], ph[j, p]) + dot_nn(wh[p], pw[j, p]) + dot_nn(wl[p], ph[j, p])
            total = term if total is None else total + term
        rbuf[2 * j] = total[:, :WIDTH]
        rbuf[2 * j + 1] = total[:, WIDTH:]

    def r_arrival(t, h):
        peer = (r + slice_offset(t)) % ROWS
        rows = pl.ds(h * half_rows, half_rows)
        i = 2 * t + h
        return remote(rbuf.at[t, rows], resp_ref.at[peer, rows], rs.at[i], rr.at[i], peer, c)

    def d_copy(src, dst, n, row, column):
        return remote(src, dst, ds.at[n], dr.at[n], row, column)

    def stage1():
        return d_copy(d1.at[pl.ds((1 - k) * half_rows, half_rows)], d1r, 0, r, col(x, y, 1 - k))

    def stage2(d):
        to = (y + d) % 4
        return d_copy(d2.at[pl.ds(to * 64, 64)], d2r.at[d - 1], d, r, col(x, to, k))

    def stage3(d):
        to = (x + d) % 4
        return d_copy(d3.at[pl.ds(to * 16, 16)], d3r.at[d - 1], 3 + d, r, col(to, y, k))

    def tile(ref, base, row):
        return ref.at[pl.ds(base + (row // 4) * 8, 8), pl.ds((row % 4) * 128, 128)]

    def stage4(d):
        to = (r + d) % ROWS
        return d_copy(tile(d4, 0, to), d4r.at[d - 1], 6 + d, to, c)

    base3 = k * 256 + y * 64 + x * 16
    base2 = k * 256 + y * 64
    base1 = k * 256

    def back4(d, arriving=False):
        to = (r + d) % ROWS
        where = tile(g, base3, (r - d + ROWS) % ROWS if arriving else r)
        return d_copy(where, where, 13 + d, to, c)

    def back3(d, arriving=False):
        source = (x - d + 4) % 4 if arriving else x
        where = g.at[pl.ds(base2 + source * 16, 16)]
        return d_copy(where, where, 20 + d, r, col((x + d) % 4, y, k))

    def back2(d, arriving=False):
        source = (y - d + 4) % 4 if arriving else y
        where = g.at[pl.ds(base1 + source * 64, 64)]
        return d_copy(where, where, 23 + d, r, col(x, (y + d) % 4, k))

    def back1(arriving=False):
        where = g.at[pl.ds((1 - k if arriving else k) * 256, 256)]
        return d_copy(where, where, 27, r, col(x, y, 1 - k))

    response(1)
    r_send(2)
    r_send(3)

    @pl.loop(0, NPANEL)
    def _(p):
        term = dot_nt(wh[p], ah[p]) + dot_nt(wh[p], al[p]) + dot_nt(wl[p], ah[p])

        @pl.when(p == 0)
        def _():
            d1[...] = term

        @pl.when(p > 0)
        def _():
            d1[...] += term

    stage1().start()
    response(0)
    r_send(1)
    keep = pltpu.make_async_copy(rbuf.at[0], resp_ref.at[r], loc.at[0])
    keep.start()
    stage1().wait_recv()
    d2[...] = d1[pl.ds(k * half_rows, half_rows), :] + d1r[...]
    for d in range(1, 4):
        stage2(d).start()
    response(2)
    r_send(4)
    response(3)
    @pl.loop(0, STEPS)
    def _(i):
        @pl.when(i >= CHUNKS)
        def _():
            z_copy(i // CHUNKS, i % CHUNKS).wait_send()

        @pl.when(y < 2)
        def _():
            @pl.when(x == 0)
            def _():
                x_out(i, 1, xs1).wait_send()
                x_out(i, 3, xs2).wait_send()

            @pl.when((x == 1) | (x == 3))
            def _():
                x_half(i, x // 2).wait_send()

            y_two(first, i).wait_send()

        y_one(first, i).wait_send()
        core(first, i, cs1, cr1).wait_send()
        core(second, i, cs2, cr2).wait_send()

    for d in range(1, 4):
        stage2(d).wait_recv()
    d3[...] = d2[pl.ds(y * 64, 64), :] + d2r[0] + d2r[1] + d2r[2]
    for d in range(1, 4):
        stage3(d).start()
    for d in range(1, 4):
        stage3(d).wait_recv()
    d4[...] = d3[pl.ds(x * 16, 16), :] + d3r[0] + d3r[1] + d3r[2]
    for d in range(1, ROWS):
        stage4(d).start()
    for d in range(1, ROWS):
        stage4(d).wait_recv()
    mine = d4[pl.ds((r // 4) * 8, 8), pl.ds((r % 4) * 128, 128)]
    for d in range(1, ROWS):
        mine = mine + d4r[d - 1]
    g[pl.ds(base3 + (r // 4) * 8, 8), pl.ds((r % 4) * 128, 128)] = mine * (1.0 / 256.0)
    for d in range(1, ROWS):
        back4(d).start()
    r_send(7)
    r_send(5)
    r_send(6)
    for d in range(1, ROWS):
        back4(d, True).wait_recv()
    for d in range(1, 4):
        back3(d).start()
    for d in range(1, 4):
        back3(d, True).wait_recv()
    for d in range(1, 4):
        back2(d).start()
    for d in range(1, 4):
        back2(d, True).wait_recv()
    back1().start()
    back1(True).wait_recv()
    out = pltpu.make_async_copy(g, dens_ref, loc.at[1])
    out.start()

    keep.wait()
    for t in range(1, ROWS):
        for h in range(2):
            r_arrival(t, h).wait_recv()
    out.wait()
    for t in range(1, ROWS):
        for h in range(2):
            r_copy(t, h).wait_send()
    stage1().wait_send()
    back1().wait_send()
    for d in range(1, 4):
        stage2(d).wait_send()
        stage3(d).wait_send()
        back3(d).wait_send()
        back2(d).wait_send()
    for d in range(1, ROWS):
        stage4(d).wait_send()
        back4(d).wait_send()


def on_device(three_index, occ_energy, vir_energy, block_mask, pair_list):
    any_space = pl.BlockSpec(memory_space=pl.ANY)
    vmem = pl.BlockSpec(memory_space=pltpu.VMEM)
    smem = pl.BlockSpec(memory_space=pltpu.SMEM)
    dma = pltpu.SemaphoreType.DMA
    square = (NPANEL, NVIR, NVIR)
    return pl.pallas_call(
        kernel,
        out_shape=(
            jax.ShapeDtypeStruct((ROWS, NVIR, WIDTH), F32),
            jax.ShapeDtypeStruct((NVIR, NVIR), F32),
        ),
        in_specs=[any_space, smem, vmem, any_space, smem],
        out_specs=(any_space, any_space),
        scratch_shapes=[
            pltpu.VMEM((NPANEL + 1, ROWS, NVIR, WIDTH), F32),
            pltpu.VMEM((8, 16, ROWS * COLS), jnp.int32),
            pltpu.VMEM((ROWS, NPANEL + 1, 8, WIDTH), F32),
            pltpu.VMEM((NVIR, 128), F32),
            pltpu.VMEM((4, NVIR, 2 * WIDTH), BF16),
            pltpu.VMEM((4, NVIR, 2 * WIDTH), BF16),
            pltpu.VMEM((4, NPANEL, NVIR, 2 * WIDTH), BF16),
            pltpu.VMEM((4, NPANEL, NVIR, 2 * WIDTH), BF16),
            pltpu.VMEM(square, F32),
            pltpu.VMEM(square, F32),
            pltpu.VMEM(square, BF16),
            pltpu.VMEM(square, BF16),
            pltpu.VMEM(square, BF16),
            pltpu.VMEM(square, BF16),
            pltpu.VMEM((ROWS, NVIR, WIDTH), F32),
            pltpu.VMEM((512, NVIR), F32),
            pltpu.VMEM((256, NVIR), F32),
            pltpu.VMEM((256, NVIR), F32),
            pltpu.VMEM((3, 64, NVIR), F32),
            pltpu.VMEM((64, NVIR), F32),
            pltpu.VMEM((3, 16, NVIR), F32),
            pltpu.VMEM((16, NVIR), F32),
            pltpu.VMEM((7, 8, 128), F32),
            pltpu.VMEM((NVIR, NVIR), F32),
            dma((STEPS,)), dma((STEPS,)),
            dma((STEPS,)), dma((STEPS,)), dma((STEPS,)), dma((STEPS, 2)),
            dma((STEPS,)), dma((STEPS,)), dma((STEPS,)), dma((STEPS,)),
            dma((STEPS,)), dma((STEPS,)), dma((STEPS,)), dma((STEPS,)),
            dma((2 * ROWS,)), dma((2 * ROWS,)), dma((28,)), dma((28,)), dma((2,)),
        ],
        compiler_params=pltpu.CompilerParams(
            collective_id=0, has_side_effects=True, vmem_limit_bytes=VMEM_LIMIT
        ),
    )(
        three_index, occ_energy, vir_energy[None, :], block_mask.transpose(1, 2, 0), pair_list.T
    )


def solution(mesh):
    placed = (P("col", None, "row"), P(), P(), P(), P("col", None))
    return jax.shard_map(
        on_device,
        mesh=mesh,
        in_specs=placed,
        out_specs=(P("col", None, "row"), P()),
        check_vma=False,
    )
```

```python
import jax
import jax.numpy as jnp
from jax import lax
from jax.experimental import pallas as pl
from jax.experimental.pallas import tpu as pltpu
from jax.sharding import PartitionSpec as P

NVIR = 512
NAUX = 1024
BLOCK = 64
PAIRS_DEV = 4
NPANEL = 4
ROWS = 8
COLS = 32
WIDTH = NAUX // ROWS
CHUNKS = 4
PIECE = NVIR // CHUNKS
STEPS = ROWS * CHUNKS
PER_UNIT = CHUNKS // 2
LAG = 3
BEHIND = (LAG + PER_UNIT - 2) // PER_UNIT
VMEM_LIMIT = 50 * 1024 * 1024
MESH = pl.DeviceIdType.MESH
F32 = jnp.float32
BF16 = jnp.bfloat16


def dot_nt(a, b):
    return lax.dot_general(a, b, (((1,), (1,)), ((), ())), preferred_element_type=F32)


def dot_nn(a, b):
    return lax.dot_general(a, b, (((1,), (0,)), ((), ())), preferred_element_type=F32)


def split(x):
    high = x.astype(BF16)
    return high, (x - high.astype(F32)).astype(BF16)


def slice_offset(t):
    return jnp.where(t % 2 == 1, (t + 1) // 2, ROWS - t // 2)


def kernel(
    x_ref, occ_ref, vir_ref, mask_ref, pair_ref,
    resp_ref, dens_ref,
    buf, mbuf, maskx, vcol, oh, ol, ph, pw, acc, recip, ah, al, wh, wl, rbuf,
    d1, d1r, d2, d2r, d3, d3r, d4, d4r, g,
    zs, zr, xs1, xs2, xr1, xr2, ys1, yr1, ys2, yr2, cs1, cr1, cs2, cr2,
    rs, rr, ds, dr, loc,
):
    r = lax.axis_index("row")
    c = lax.axis_index("col")
    x, y, k = c // 8, (c // 2) % 4, c % 2

    def col(xx, yy, kk):
        return (xx * 4 + yy) * 2 + kk

    own = jnp.where(c < NPANEL, c, NPANEL)
    first = k + 2 * jnp.where((y == 1) | (y == 2), 1, 0)
    second = k + 2 - 2 * jnp.where((y == 1) | (y == 2), 1, 0)
    y1, y2 = y + 1 - 2 * (y % 2), 3 - y

    half_rows = NVIR // 2

    def remote(src, dst, ssem, rsem, row, column):
        return pltpu.make_async_remote_copy(
            src_ref=src, dst_ref=dst, send_sem=ssem, recv_sem=rsem,
            device_id=(row, column), device_id_type=MESH,
        )

    barrier = pltpu.get_barrier_semaphore()
    for d in range(1, ROWS):
        pl.semaphore_signal(barrier, inc=1, device_id=((r + d) % ROWS, c), device_id_type=MESH)
    for d in range(1, 4):
        pl.semaphore_signal(barrier, inc=1, device_id=(r, col((x + d) % 4, y, k)), device_id_type=MESH)
        pl.semaphore_signal(barrier, inc=1, device_id=(r, col(x, (y + d) % 4, k)), device_id_type=MESH)
    pl.semaphore_signal(barrier, inc=1, device_id=(r, col(x, y, 1 - k)), device_id_type=MESH)

    local = pltpu.make_async_copy(x_ref.at[r], buf.at[own, 0], loc.at[0])
    local.start()
    mask_copy = pltpu.make_async_copy(mask_ref, mbuf, loc.at[1])
    mask_copy.start()
    pl.semaphore_wait(barrier, 14)

    def z_copy(t, ch):
        rows = pl.ds(ch * PIECE, PIECE)
        peer = (r + slice_offset(t)) % ROWS
        i = t * CHUNKS + ch
        return remote(x_ref.at[peer, rows], buf.at[own, t, rows], zs.at[i], zr.at[i], peer, c)

    @pl.loop(CHUNKS, STEPS)
    def _(i):
        z_copy(i // CHUNKS, i % CHUNKS).start()

    def piece(q, i):
        return buf.at[q, i // CHUNKS, pl.ds((i % CHUNKS) * PIECE, PIECE)]

    def half(q, i, h):
        return buf.at[q, i // CHUNKS, pl.ds((i % CHUNKS) * PIECE + h * (PIECE // 2), PIECE // 2)]

    def x_out(i, to, ssem):
        return remote(piece(first, i), piece(first, i), ssem.at[i], xr1.at[i], r, col(to, y, k))

    def x_half(i, h):
        return remote(half(first, i, h), half(first, i, h), xs1.at[i], xr2.at[i, h], r, col(2, y, k))

    def y_one(q, i):
        return remote(piece(q, i), piece(q, i), ys1.at[i], yr1.at[i], r, col(x, y1, k))

    def y_two(q, i):
        return remote(piece(q, i), piece(q, i), ys2.at[i], yr2.at[i], r, col(x, y2, k))

    def core(q, i, ssem, rsem):
        return remote(piece(q, i), piece(q, i), ssem.at[i], rsem.at[i], r, col(x, y, 1 - k))

    def wait_z(i):
        @pl.when(i >= CHUNKS)
        def _():
            z_copy(i // CHUNKS, i % CHUNKS).wait_recv()

    def send_first(i):
        @pl.when(y < 2)
        def _():
            @pl.when(x == 0)
            def _():
                wait_z(i)
                x_out(i, 1, xs1).start()
                x_out(i, 3, xs2).start()

            @pl.when(x == 1)
            def _():
                x_out(i, 1, xs1).wait_recv()
                x_half(i, 0).start()

            @pl.when(x == 3)
            def _():
                x_out(i, 3, xs1).wait_recv()
                x_half(i, 1).start()

            @pl.when(x == 2)
            def _():
                x_half(i, 0).wait_recv()
                x_half(i, 1).wait_recv()

            y_two(first, i).start()

        @pl.when(y >= 2)
        def _():
            y_two(first, i).wait_recv()

        y_one(first, i).start()
        core(first, i, cs1, cr1).start()

    def send_second(i):
        y_one(second, i).wait_recv()
        core(second, i, cs2, cr2).start()

    def arrived(i):
        core(first + 1 - 2 * k, i, cs1, cr1).wait_recv()
        core(second + 1 - 2 * k, i, cs2, cr2).wait_recv()

    local.wait()
    send_first(0)

    mask_copy.wait()
    flat = mbuf[...].reshape(ROWS * 2 * ROWS, ROWS * COLS).astype(F32).astype(BF16)
    index = lax.broadcasted_iota(jnp.int32, (8, ROWS * COLS), 0)
    orbital = lax.broadcasted_iota(jnp.int32, (8, ROWS * COLS), 1)
    wanted = ROWS * jnp.where(index < NPANEL, index, c) + r
    picked = dot_nt((orbital == wanted).astype(F32).astype(BF16), flat)
    block_of = lax.broadcasted_iota(jnp.int32, (8, 128), 1) >> 4
    band = lax.broadcasted_iota(jnp.int32, (8, 128), 0)
    masks = jnp.concatenate(
        [jnp.where(block_of == band, picked[n:n + 1, :], 0.0) for n in range(NPANEL + 1)], axis=0
    ).astype(BF16)
    block = lax.broadcasted_iota(jnp.int32, (128, WIDTH), 0) & 15
    lane = lax.broadcasted_iota(jnp.int32, (128, WIDTH), 1) >> 6
    for t in range(ROWS):
        s = (r - slice_offset(t) + ROWS) % ROWS
        wide = dot_nn(masks, (block == 2 * s + lane).astype(F32).astype(BF16))
        for n in range(NPANEL + 1):
            maskx[t, n] = wide[n * 8:(n + 1) * 8]
    for a in range(0, NVIR, 128):
        vcol[a:a + 128, :] = jnp.broadcast_to(vir_ref[:, a:a + 128], (128, 128)).T

    def set_recip(p):
        pair = occ_ref[ROWS * c + r] + occ_ref[ROWS * p + r]
        live = jnp.float32(0.0)
        for s in range(PAIRS_DEV):
            live = jnp.where(pair_ref[s, r] == p, jnp.float32(1.0), live)
        for a in range(0, NVIR, 128):
            for b in range(0, NVIR, 128):
                recip[p, a:a + 128, b:b + 128] = live / (
                    pair - vcol[a:a + 128, :] - vir_ref[:, b:b + 128]
                )

    def convert(j, q, index, hi_ref, lo_ref):
        for h in range(2):
            t = 2 * j + h
            rows = maskx[t, index]
            for b in range(NVIR // BLOCK):
                a = slice(b * BLOCK, (b + 1) * BLOCK)
                high, low = split(buf[q, t, a, :] * rows[b:b + 1, :])
                hi_ref[a, h * WIDTH:(h + 1) * WIDTH] = high
                lo_ref[a, h * WIDTH:(h + 1) * WIDTH] = low

    def cross(j, p):
        convert(j, p, p, ph.at[j, p], pw.at[j, p])
        term = dot_nt(oh[j], ph[j, p]) + dot_nt(oh[j], pw[j, p]) + dot_nt(ol[j], ph[j, p])

        @pl.when(j == 0)
        def _():
            acc[p] = term

        @pl.when(j > 0)
        def _():
            acc[p] += term

    def pair_arrived(j):
        @pl.loop(0, 2 * CHUNKS)
        def _(n):
            i = j * 2 * CHUNKS + n

            @pl.when(jnp.logical_not((x == 0) & (y < 2)))
            def _():
                wait_z(i)

            arrived(i)

        convert(j, own, NPANEL, oh.at[j], ol.at[j])

    @pl.loop(0, 4 * NPANEL + 4 + BEHIND)
    def _(v):
        for m in range(PER_UNIT):
            i = v * PER_UNIT + m

            @pl.when(i + 1 < STEPS)
            def _():
                send_first(i + 1)

            late = i + 1 - LAG

            @pl.when((late >= 0) & (late < STEPS))
            def _():
                send_second(late)

        @pl.when(v < NPANEL)
        def _():
            set_recip(v)

        unit = v - 4 - BEHIND

        @pl.when((unit >= 0) & (unit < 4 * NPANEL))
        def _():
            @pl.when(unit % 4 == 0)
            def _():
                pair_arrived(unit // 4)

            cross(unit // 4, unit % 4)

    @pl.loop(0, NPANEL)
    def _(p):
        for a in range(0, NVIR, 128):
            rows = slice(a, a + 128)
            here = acc[p, rows, :]
            turned = acc[p, :, rows].T
            scale = recip[p, rows, :]
            amplitude = here * scale
            high, low = split(amplitude)
            ah[p, rows, :] = high
            al[p, rows, :] = low
            high, low = split(2.0 * amplitude - turned * scale)
            wh[p, rows, :] = high
            wl[p, rows, :] = low

    def r_copy(t, h):
        peer = (r - slice_offset(t) + ROWS) % ROWS
        rows = pl.ds(h * half_rows, half_rows)
        i = 2 * t + h
        return remote(rbuf.at[t, rows], resp_ref.at[r, rows], rs.at[i], rr.at[i], peer, c)

    def r_send(t):
        for h in range(2):
            r_copy(t, h).start()

    def response(j):
        total = None
        for p in range(NPANEL):
            term = dot_nn(wh[p], ph[j, p]) + dot_nn(wh[p], pw[j, p]) + dot_nn(wl[p], ph[j, p])
            total = term if total is None else total + term
        rbuf[2 * j] = total[:, :WIDTH]
        rbuf[2 * j + 1] = total[:, WIDTH:]

    def r_arrival(t, h):
        peer = (r + slice_offset(t)) % ROWS
        rows = pl.ds(h * half_rows, half_rows)
        i = 2 * t + h
        return remote(rbuf.at[t, rows], resp_ref.at[peer, rows], rs.at[i], rr.at[i], peer, c)

    def d_copy(src, dst, n, row, column):
        return remote(src, dst, ds.at[n], dr.at[n], row, column)

    def stage1():
        return d_copy(d1.at[pl.ds((1 - k) * half_rows, half_rows)], d1r, 0, r, col(x, y, 1 - k))

    def stage2(d):
        to = (y + d) % 4
        return d_copy(d2.at[pl.ds(to * 64, 64)], d2r.at[d - 1], d, r, col(x, to, k))

    def stage3(d):
        to = (x + d) % 4
        return d_copy(d3.at[pl.ds(to * 16, 16)], d3r.at[d - 1], 3 + d, r, col(to, y, k))

    def tile(ref, base, row):
        return ref.at[pl.ds(base + (row // 4) * 8, 8), pl.ds((row % 4) * 128, 128)]

    def stage4(d):
        to = (r + d) % ROWS
        return d_copy(tile(d4, 0, to), d4r.at[d - 1], 6 + d, to, c)

    base3 = k * 256 + y * 64 + x * 16
    base2 = k * 256 + y * 64
    base1 = k * 256

    def back4(d, arriving=False):
        to = (r + d) % ROWS
        where = tile(g, base3, (r - d + ROWS) % ROWS if arriving else r)
        return d_copy(where, where, 13 + d, to, c)

    def back3(d, arriving=False):
        source = (x - d + 4) % 4 if arriving else x
        where = g.at[pl.ds(base2 + source * 16, 16)]
        return d_copy(where, where, 20 + d, r, col((x + d) % 4, y, k))

    def back2(d, arriving=False):
        source = (y - d + 4) % 4 if arriving else y
        where = g.at[pl.ds(base1 + source * 64, 64)]
        return d_copy(where, where, 23 + d, r, col(x, (y + d) % 4, k))

    def back1(arriving=False):
        where = g.at[pl.ds((1 - k if arriving else k) * 256, 256)]
        return d_copy(where, where, 27, r, col(x, y, 1 - k))

    response(1)
    r_send(2)
    r_send(3)

    @pl.loop(0, NPANEL)
    def _(p):
        term = dot_nt(wh[p], ah[p]) + dot_nt(wh[p], al[p]) + dot_nt(wl[p], ah[p])

        @pl.when(p == 0)
        def _():
            d1[...] = term

        @pl.when(p > 0)
        def _():
            d1[...] += term

    stage1().start()
    response(0)
    r_send(1)
    keep = pltpu.make_async_copy(rbuf.at[0], resp_ref.at[r], loc.at[0])
    keep.start()
    stage1().wait_recv()
    d2[...] = d1[pl.ds(k * half_rows, half_rows), :] + d1r[...]
    for d in range(1, 4):
        stage2(d).start()
    response(2)
    r_send(4)
    response(3)
    @pl.loop(0, STEPS)
    def _(i):
        @pl.when(i >= CHUNKS)
        def _():
            z_copy(i // CHUNKS, i % CHUNKS).wait_send()

        @pl.when(y < 2)
        def _():
            @pl.when(x == 0)
            def _():
                x_out(i, 1, xs1).wait_send()
                x_out(i, 3, xs2).wait_send()

            @pl.when((x == 1) | (x == 3))
            def _():
                x_half(i, x // 2).wait_send()

            y_two(first, i).wait_send()

        y_one(first, i).wait_send()
        core(first, i, cs1, cr1).wait_send()
        core(second, i, cs2, cr2).wait_send()

    for d in range(1, 4):
        stage2(d).wait_recv()
    r_copy(5, 0).start()
    r_copy(6, 0).start()
    d3[...] = d2[pl.ds(y * 64, 64), :] + d2r[0] + d2r[1] + d2r[2]
    for d in range(1, 4):
        stage3(d).start()
    for d in range(1, 4):
        stage3(d).wait_recv()
    d4[...] = d3[pl.ds(x * 16, 16), :] + d3r[0] + d3r[1] + d3r[2]
    for d in range(1, ROWS):
        stage4(d).start()
    for d in range(1, ROWS):
        stage4(d).wait_recv()
    mine = d4[pl.ds((r // 4) * 8, 8), pl.ds((r % 4) * 128, 128)]
    for d in range(1, ROWS):
        mine = mine + d4r[d - 1]
    g[pl.ds(base3 + (r // 4) * 8, 8), pl.ds((r % 4) * 128, 128)] = mine * (1.0 / 256.0)
    for d in range(1, ROWS):
        back4(d).start()
    r_copy(5, 1).start()
    r_copy(6, 1).start()
    r_send(7)
    for d in range(1, ROWS):
        back4(d, True).wait_recv()
    for d in range(1, 4):
        back3(d).start()
    for d in range(1, 4):
        back3(d, True).wait_recv()
    for d in range(1, 4):
        back2(d).start()
    for d in range(1, 4):
        back2(d, True).wait_recv()
    back1().start()
    back1(True).wait_recv()
    out = pltpu.make_async_copy(g, dens_ref, loc.at[1])
    out.start()

    keep.wait()
    for t in range(1, ROWS):
        for h in range(2):
            r_arrival(t, h).wait_recv()
    out.wait()
    for t in range(1, ROWS):
        for h in range(2):
            r_copy(t, h).wait_send()
    stage1().wait_send()
    back1().wait_send()
    for d in range(1, 4):
        stage2(d).wait_send()
        stage3(d).wait_send()
        back3(d).wait_send()
        back2(d).wait_send()
    for d in range(1, ROWS):
        stage4(d).wait_send()
        back4(d).wait_send()


def on_device(three_index, occ_energy, vir_energy, block_mask, pair_list):
    any_space = pl.BlockSpec(memory_space=pl.ANY)
    vmem = pl.BlockSpec(memory_space=pltpu.VMEM)
    smem = pl.BlockSpec(memory_space=pltpu.SMEM)
    dma = pltpu.SemaphoreType.DMA
    square = (NPANEL, NVIR, NVIR)
    return pl.pallas_call(
        kernel,
        out_shape=(
            jax.ShapeDtypeStruct((ROWS, NVIR, WIDTH), F32),
            jax.ShapeDtypeStruct((NVIR, NVIR), F32),
        ),
        in_specs=[any_space, smem, vmem, any_space, smem],
        out_specs=(any_space, any_space),
        scratch_shapes=[
            pltpu.VMEM((NPANEL + 1, ROWS, NVIR, WIDTH), F32),
            pltpu.VMEM((8, 16, ROWS * COLS), jnp.int32),
            pltpu.VMEM((ROWS, NPANEL + 1, 8, WIDTH), F32),
            pltpu.VMEM((NVIR, 128), F32),
            pltpu.VMEM((4, NVIR, 2 * WIDTH), BF16),
            pltpu.VMEM((4, NVIR, 2 * WIDTH), BF16),
            pltpu.VMEM((4, NPANEL, NVIR, 2 * WIDTH), BF16),
            pltpu.VMEM((4, NPANEL, NVIR, 2 * WIDTH), BF16),
            pltpu.VMEM(square, F32),
            pltpu.VMEM(square, F32),
            pltpu.VMEM(square, BF16),
            pltpu.VMEM(square, BF16),
            pltpu.VMEM(square, BF16),
            pltpu.VMEM(square, BF16),
            pltpu.VMEM((ROWS, NVIR, WIDTH), F32),
            pltpu.VMEM((512, NVIR), F32),
            pltpu.VMEM((256, NVIR), F32),
            pltpu.VMEM((256, NVIR), F32),
            pltpu.VMEM((3, 64, NVIR), F32),
            pltpu.VMEM((64, NVIR), F32),
            pltpu.VMEM((3, 16, NVIR), F32),
            pltpu.VMEM((16, NVIR), F32),
            pltpu.VMEM((7, 8, 128), F32),
            pltpu.VMEM((NVIR, NVIR), F32),
            dma((STEPS,)), dma((STEPS,)),
            dma((STEPS,)), dma((STEPS,)), dma((STEPS,)), dma((STEPS, 2)),
            dma((STEPS,)), dma((STEPS,)), dma((STEPS,)), dma((STEPS,)),
            dma((STEPS,)), dma((STEPS,)), dma((STEPS,)), dma((STEPS,)),
            dma((2 * ROWS,)), dma((2 * ROWS,)), dma((28,)), dma((28,)), dma((2,)),
        ],
        compiler_params=pltpu.CompilerParams(
            collective_id=0, has_side_effects=True, vmem_limit_bytes=VMEM_LIMIT
        ),
    )(
        three_index, occ_energy, vir_energy[None, :], block_mask.transpose(1, 2, 0), pair_list.T
    )


def solution(mesh):
    placed = (P("col", None, "row"), P(), P(), P(), P("col", None))
    return jax.shard_map(
        on_device,
        mesh=mesh,
        in_specs=placed,
        out_specs=(P("col", None, "row"), P()),
        check_vma=False,
    )
```
